256 devices in a mesh: dp: 32 (over z, y), grp: 8 (over x, core).
Axes of the slice: x: 4, y: 4, z: 8, core: 2. Of those that a mesh axis runs over, the one named last changes fastest.
Arguments:
- tokens: bfloat16 [1024, 256, 1024], P(('dp', 'grp')), may hold values from -0.1875 to 0.1875
- patches: bfloat16 [1024, 256, 1024], P(('dp', 'grp')), may hold values from -0.1875 to 0.1875
- lengths: int32 [1024], P(('dp', 'grp')), may hold values from 16 to 256, as said below
- img_pooled: bfloat16 [1024, 1024], P(('dp', 'grp')), may hold values from -1 to 1
- txt_pooled: bfloat16 [1024, 1024], P(('dp', 'grp')), may hold values from -1 to 1
Outputs:
- grad_tokens: bfloat16 [1024, 256, 1024], P(('dp', 'grp'))
- grad_patches: bfloat16 [1024, 256, 1024], P(('dp', 'grp'))
- grad_img: bfloat16 [1024, 1024], P(('dp', 'grp'))
- grad_txt: bfloat16 [1024, 1024], P(('dp', 'grp'))
- loss_mean: float32 [], replicated
The draws below stay inside these ranges and needn't reach their ends.
Inputs may be any that keep to these rules, and one draw needn't show every extreme that they name: `lengths`: among the pairs of one index of dp (8 devices along grp), exactly 8 captions have more than 128 tokens; no device holds more than two of them and some device holds two; some caption has exactly 256 tokens and some exactly 128.
All inputs are finite; a program needn't handle non-finite values.
Results may differ from the reference program's by a relative error of at most 0.013.
Values may be sent and summed in bfloat16 or wider, within the bound.
A program may use at most 128 MiB of HBM per device.

```python
import jax
import jax.numpy as jnp
from jax import lax

D = 1024
P_SIZE = 256
LMAX = 256
PAIRS_DEV = 4
PAIRS = 1024
N_DP = 32
N_GRP = 8


def draw_lengths(key, part):
    members = N_GRP
    slots_dev = PAIRS_DEV
    group_keys = jax.random.split(key, N_DP)

    def one_group(group_key):
        key_a, key_b, key_c, key_d, key_e = jax.random.split(group_key, 5)
        donors = jax.random.randint(key_a, (), 1, members // 2 + 1)
        position = jnp.arange(members)
        pattern = jnp.where(position < donors, 2, jnp.where(position < 2 * donors, 0, 1))
        pattern = jax.random.permutation(key_b, pattern)
        slot_keys = jax.random.split(key_c, members)
        slot_rank = jax.vmap(lambda slot_key: jax.random.permutation(slot_key, slots_dev))(slot_keys)
        is_long = (slot_rank < pattern[:, None]).reshape(-1).astype(jnp.int32)
        long_len = jax.random.randint(key_d, (members * slots_dev,), LMAX // 2 + 1, LMAX + 1)
        short_len = jax.random.randint(key_e, (members * slots_dev,), LMAX // 16, LMAX // 2 + 1)
        picked = jnp.where(is_long == 1, long_len, short_len)
        index_all = jnp.arange(members * slots_dev)
        first_long = jnp.argmax(is_long)
        first_short = jnp.argmax(1 - is_long)
        picked = jnp.where(index_all == first_long, LMAX, picked)
        picked = jnp.where(index_all == first_short, LMAX // 2, picked)
        return picked
    return jax.vmap(one_group)(group_keys).reshape(-1).astype(jnp.int32)


def pooled_pair(key):
    key_img, key_txt = jax.random.split(jax.random.fold_in(key, 7), 2)
    img_draw = jax.random.normal(key_img, (PAIRS, D), jnp.float32) * 0.03125
    noise = jax.random.normal(key_txt, (PAIRS, D), jnp.float32) * 0.03125
    ramp = jnp.arange(PAIRS, dtype=jnp.float32)[:, None] / PAIRS
    mixing = 0.15 * ramp
    txt_draw = mixing * img_draw + jnp.sqrt(1.0 - mixing * mixing) * noise
    img_draw = jnp.clip(img_draw, -1.0, 1.0)
    txt_draw = jnp.clip(txt_draw, -1.0, 1.0)
    return (img_draw, txt_draw)


def draw_img_pooled(key, part):
    return pooled_pair(key)[0].astype(jnp.bfloat16)


def draw_txt_pooled(key, part):
    return pooled_pair(key)[1].astype(jnp.bfloat16)


def steps_of(own_key, shape, cuts, least, high):
    loudness = 1.0
    for dim, blocks in cuts:
        heights = jax.random.uniform(jax.random.fold_in(jax.random.fold_in(own_key, 6), dim), (blocks,), jnp.float32, least / len(cuts), high / len(cuts))
        loudness = loudness * jnp.repeat(jnp.exp(heights), shape[dim] // blocks).reshape((-1,) + (1,) * (len(shape) - 1 - dim))
    return loudness


def bell_draw(key, shape, spread, most, cuts=(), kind=jnp.bfloat16):
    entries = spread * jax.random.normal(key, shape, jnp.float32)
    if cuts:
        entries = entries * steps_of(key, shape, cuts, -0.22, 0.18)
    return jnp.clip(entries, -most, most).astype(kind)


def setup_inputs(seed: int = 0) -> dict:
    seeds = jax.random.split(jax.random.key(seed), 6)
    return {
        "tokens": bell_draw(seeds[0], (PAIRS, LMAX, D), 0.03125, 0.1875, ((0, 256),)),
        "patches": bell_draw(seeds[1], (PAIRS, P_SIZE, D), 0.03125, 0.1875, ((0, 256),)),
        "lengths": draw_lengths(jax.random.fold_in(seeds[5], 71), 0),
        "img_pooled": draw_img_pooled(jax.random.fold_in(seeds[5], 71), 0),
        "txt_pooled": draw_txt_pooled(jax.random.fold_in(seeds[5], 71), 0),
    }


RANGE_EPS = 1e-06
NORM_EPS = 1e-06
GLOBAL_SCALE = 100.0
FINE_SCALE = 50.0
MASK_FILL = -1000000000.0

def pair_terms(tok_rows, patch_rows, length):
    patch_count = patch_rows.shape[0]
    slot_count = tok_rows.shape[0]
    similar = jnp.dot(tok_rows, patch_rows.T, preferred_element_type=jnp.float32)
    lowest = lax.optimization_barrier(jnp.min(similar, 1, keepdims=True))
    highest = lax.optimization_barrier(jnp.max(similar, 1, keepdims=True))
    scaled = (similar - lowest) / (highest - lowest + RANGE_EPS)
    weights = jnp.maximum(scaled - 1.0 / patch_count, 0.0)
    weights = weights / lax.optimization_barrier(jnp.sum(weights, 1, keepdims=True))
    grouped = jnp.dot(weights.astype(jnp.bfloat16), patch_rows, preferred_element_type=jnp.float32)
    group_unit = grouped * lax.rsqrt(lax.optimization_barrier(jnp.sum(grouped * grouped, 1, keepdims=True)) + NORM_EPS)
    token_float = tok_rows.astype(jnp.float32)
    token_unit = token_float * lax.rsqrt(lax.optimization_barrier(jnp.sum(token_float * token_float, 1, keepdims=True)) + NORM_EPS)
    logits = FINE_SCALE * jnp.dot(group_unit.astype(jnp.bfloat16), token_unit.astype(jnp.bfloat16).T, preferred_element_type=jnp.float32)
    position = jnp.arange(slot_count, dtype=jnp.int32)
    valid = position < length
    both_valid = jnp.logical_and(valid[:, None], valid[None, :])
    masked = jnp.where(both_valid, logits, MASK_FILL)
    row_lse = jax.nn.logsumexp(masked, 1)
    col_lse = jax.nn.logsumexp(masked, 0)
    per_token = jnp.where(valid, row_lse + col_lse - 2.0 * jnp.diagonal(logits), 0.0)
    return jnp.sum(per_token) / (2.0 * length.astype(jnp.float32))

def pair_grads(tok_rows, patch_rows, length):

    def closure(first_arg, second_arg):
        return pair_terms(first_arg, second_arg, length)
    value, pullback = jax.vjp(closure, tok_rows, patch_rows)
    grad_tok, grad_patch = pullback(jnp.ones((), jnp.float32))
    return (value, grad_tok, grad_patch)

def unit_rows(pooled):
    values = pooled.astype(jnp.float32)
    inverse = lax.rsqrt(lax.optimization_barrier(jnp.sum(values * values, -1, keepdims=True)) + NORM_EPS)
    return (values * inverse, inverse)

def reference(tokens, patches, lengths, img_pooled, txt_pooled):
    values, grad_tokens, grad_patches = lax.map(lambda packed: pair_grads(packed[0], packed[1], packed[2]), (tokens, patches, lengths))
    fine_total = jnp.sum(values)
    img_unit, img_inverse = unit_rows(img_pooled)
    txt_unit, txt_inverse = unit_rows(txt_pooled)
    img_half = img_unit.astype(jnp.bfloat16)
    txt_half = txt_unit.astype(jnp.bfloat16)
    pair_total = img_half.shape[0]
    logits = GLOBAL_SCALE * jnp.dot(img_half, txt_half.T, preferred_element_type=jnp.float32)
    row_lse = jax.nn.logsumexp(logits, 1)
    col_lse = jax.nn.logsumexp(logits, 0)
    matches = GLOBAL_SCALE * lax.optimization_barrier(jnp.sum(img_half.astype(jnp.float32) * txt_half.astype(jnp.float32), -1))
    global_total = 0.5 * jnp.sum(row_lse + col_lse - 2.0 * matches)
    identity = jnp.eye(pair_total, dtype=jnp.float32)
    row_part = (0.5 * jnp.exp(logits - row_lse[:, None]) - 0.5 * identity).astype(jnp.bfloat16)
    col_part = (0.5 * jnp.exp(logits - col_lse[None, :]) - 0.5 * identity).astype(jnp.bfloat16)
    img_dir = GLOBAL_SCALE * (jnp.dot(row_part, txt_half, preferred_element_type=jnp.float32) + jnp.dot(col_part, txt_half, preferred_element_type=jnp.float32))
    txt_dir = GLOBAL_SCALE * (jnp.dot(row_part.T, img_half, preferred_element_type=jnp.float32) + jnp.dot(col_part.T, img_half, preferred_element_type=jnp.float32))
    grad_img = ((img_dir - img_unit * lax.optimization_barrier(jnp.sum(img_unit * img_dir, -1, keepdims=True))) * img_inverse).astype(jnp.bfloat16)
    grad_txt = ((txt_dir - txt_unit * lax.optimization_barrier(jnp.sum(txt_unit * txt_dir, -1, keepdims=True))) * txt_inverse).astype(jnp.bfloat16)
    loss_mean = (global_total + fine_total) / pair_total
    return (grad_tokens, grad_patches, grad_img, grad_txt, loss_mean)
```

```python
import functools

import jax
import jax.numpy as jnp
from jax import lax
from jax.experimental import pallas as pl
from jax.experimental.pallas import tpu as pltpu
from jax.sharding import PartitionSpec as P

MESH = pl.DeviceIdType.MESH
F32 = jnp.float32
BF16 = jnp.bfloat16

RANGE_EPS = 1e-06
NORM_EPS = 1e-06
GLOBAL_SCALE = 100.0
FINE_SCALE = 50.0

NX, NY, NZ, NC = 4, 4, 8, 2
GROUP = 16
D = 1024
CH = D // 128
PAIRS = 4
ROWS = GROUP * PAIRS
SLOT = PAIRS * CH
T = 256
BLK = 64


def dot_nn(a, b):
    return lax.dot_general(a, b, (((1,), (0,)), ((), ())), preferred_element_type=F32)


def dot_nt(a, b):
    return lax.dot_general(a, b, (((1,), (1,)), ((), ())), preferred_element_type=F32)


def dot_tn(a, b):
    return lax.dot_general(a, b, (((0,), (0,)), ((), ())), preferred_element_type=F32)


def ring(d, n):
    return min(d, n - d)


A_OFFS = sorted(
    ((dx, dy) for dx in range(NX) for dy in range(NY) if (dx, dy) != (0, 0)),
    key=lambda o: -(ring(o[0], NX) + ring(o[1], NY)),
)
B_OFFS = sorted(
    ((dz, dc) for dz in range(NZ) for dc in range(NC) if (dz, dc) != (0, 0)),
    key=lambda o: -ring(o[0], NZ),
)


def fine_pair(pair, length, tok, pat, s_ref, q_ref, hi_ref, lo_ref, wb_ref, wq_ref, z_ref,
              e_ref, bp_ref, v_ref, x1_ref, d_ref, col_ref, ds_out, m_out, c_out):
    s_ref[...] = dot_nt(tok[...], pat[...])
    q_ref[...] = dot_nt(pat[...], pat[...]).astype(BF16)
    inv_len = 0.5 / jnp.full((1, 1), length, jnp.int32).astype(F32)

    for b in range(T // BLK):
        rows = pl.ds(b * BLK, BLK)
        s = s_ref[rows, :]
        low = jnp.min(s, 1, keepdims=True)
        high = jnp.max(s, 1, keepdims=True)
        inv = 1.0 / (high - low + RANGE_EPS)
        x = (s - low) * inv - 1.0 / T
        raw = jnp.maximum(x, 0.0)
        iw = 1.0 / jnp.sum(raw, 1, keepdims=True)
        wb_ref[rows, :] = (raw * iw).astype(BF16)
        tf = tok[rows, :].astype(F32)
        ti = lax.rsqrt(jnp.sum(tf * tf, 1, keepdims=True) + NORM_EPS)
        sp = s * ti
        hi = sp.astype(BF16)
        hi_ref[rows, :] = hi
        lo_ref[rows, :] = (sp - hi.astype(F32)).astype(BF16)
        col_ref[rows, 0:1] = low
        col_ref[rows, 1:2] = high
        col_ref[rows, 2:3] = inv
        col_ref[rows, 3:4] = iw
        col_ref[rows, 4:5] = ti

    wq_ref[...] = dot_nn(wb_ref[...], q_ref[...])
    z_ref[...] = dot_nt(wb_ref[...], hi_ref[...]) + dot_nt(wb_ref[...], lo_ref[...])

    lane = lax.broadcasted_iota(jnp.int32, (BLK, T), 1)
    lane_ok = lane < length
    col_sum = jnp.zeros((1, T), F32)
    loss = jnp.zeros((1, 1), F32)
    for b in range(T // BLK):
        rows = pl.ds(b * BLK, BLK)
        sub = b * BLK + lax.broadcasted_iota(jnp.int32, (BLK, 1), 0)
        row_ok = sub < length
        gg = jnp.maximum(jnp.sum(wb_ref[rows, :].astype(F32) * wq_ref[rows, :], 1, keepdims=True), 0.0)
        gi = lax.rsqrt(gg + NORM_EPS)
        z = z_ref[rows, :] * (FINE_SCALE * gi)
        e = jnp.where(jnp.logical_and(lane_ok, row_ok), jnp.exp(z), 0.0)
        z_ref[rows, :] = z
        e_ref[rows, :] = e
        rs = jnp.sum(e, 1, keepdims=True)
        col_sum = col_sum + jnp.sum(e, 0, keepdims=True)
        diag = jnp.sum(jnp.where(lane == sub, z, 0.0), 1, keepdims=True)
        per_row = jnp.where(row_ok, jnp.log(rs) - 2.0 * diag, 0.0)
        loss = loss + jnp.sum(per_row, 0, keepdims=True)
        col_ref[rows, 5:6] = gi
        col_ref[rows, 6:7] = jnp.where(row_ok, 1.0 / rs, 0.0)
    lane_row = lax.broadcasted_iota(jnp.int32, (1, T), 1) < length
    loss = loss + jnp.sum(jnp.where(lane_row, jnp.log(col_sum), 0.0), 1, keepdims=True)
    ic = jnp.where(lane_row, 1.0 / col_sum, 0.0)

    for b in range(T // BLK):
        rows = pl.ds(b * BLK, BLK)
        sub = b * BLK + lax.broadcasted_iota(jnp.int32, (BLK, 1), 0)
        row_ok = sub < length
        gi = col_ref[rows, 5:6]
        ir = col_ref[rows, 6:7]
        two = jnp.where(row_ok, 2.0, 0.0)
        g = e_ref[rows, :] * (ir + ic) - jnp.where(lane == sub, two, 0.0)
        r = jnp.sum(g * z_ref[rows, :], 1, keepdims=True) * inv_len
        bp_ref[rows, :] = (g * (gi * (FINE_SCALE * inv_len))).astype(BF16)
        coef = gi * gi * r
        v_ref[rows, :] = (wb_ref[rows, :].astype(F32) * (-coef)).astype(BF16)
        col_ref[rows, 7:8] = coef

    x1_ref[...] = dot_nn(bp_ref[...], hi_ref[...]) + dot_nn(bp_ref[...], lo_ref[...])
    d_ref[...] = dot_tn(bp_ref[...], wb_ref[...])
    m_out[pair] = dot_tn(v_ref[...], wb_ref[...]).astype(BF16)

    for b in range(T // BLK):
        rows = pl.ds(b * BLK, BLK)
        low = col_ref[rows, 0:1]
        high = col_ref[rows, 1:2]
        inv = col_ref[rows, 2:3]
        iw = col_ref[rows, 3:4]
        ti = col_ref[rows, 4:5]
        coef = col_ref[rows, 7:8]
        s = s_ref[rows, :]
        x = (s - low) * inv - 1.0 / T
        w = jnp.maximum(x, 0.0) * iw
        gate = jnp.where(x > 0.0, 1.0, jnp.where(x == 0.0, 0.5, 0.0))
        dw = x1_ref[rows, :] - coef * wq_ref[rows, :]
        mean = jnp.sum(dw * w, 1, keepdims=True)
        a = gate * (dw - mean) * (iw * inv)
        total = jnp.sum(a, 1, keepdims=True)
        at_high = jnp.where(s == high, 1.0, 0.0)
        at_low = jnp.where(s == low, 1.0, 0.0)
        to_high = total * (-1.0 / T) / jnp.sum(at_high, 1, keepdims=True)
        to_low = total * (1.0 / T - 1.0) / jnp.sum(at_low, 1, keepdims=True)
        d = d_ref[rows, :] * ti
        along = jnp.sum(d * s, 1, keepdims=True)
        ds = a + at_high * to_high + at_low * to_low + d
        ds_out[pair, rows, :] = ds.astype(BF16)
        c_out[pair, rows, :] = -(ti * ti) * along
    return loss * inv_len


def unit_rows(pooled):
    values = pooled.astype(F32)
    inverse = lax.rsqrt(jnp.sum(values * values, 1, keepdims=True) + NORM_EPS)
    return values * inverse, inverse


def exchange_kernel(len_ref, tok_hbm, pat_hbm, img_ref, txt_ref,
                    ds_out, m_out, c_out, gimg_out, gtxt_out, loss_out,
                    tok_v, pat_v, s_ref, q_ref, hi_ref, lo_ref, wb_ref, wq_ref, z_ref, e_ref,
                    bp_ref, v_ref, x1_ref, d_ref, col_ref,
                    stage, unit_a, unit_b, mat_a, mat_b, wide, half_a, half_b, part_a, part_b,
                    stat_a, stat_b, lse_a, lse_b, got_a, got_b, note_a, note_b, tell_a, tell_b,
                    fine_ref, in_sem, send_sem, recv_sem):
    dp = lax.axis_index("dp")
    grp = lax.axis_index("grp")
    z, y = dp // NY, dp % NY
    x, core = grp // NC, grp % NC
    u = y * NX + x
    v = z * NC + core

    def peer_a(off):
        px, py = (x + off[0]) % NX, (y + off[1]) % NY
        return (z * NY + py, px * NC + core), py * NX + px

    def peer_b(off):
        pz, pc = (z + off[0]) % NZ, (core + off[1]) % NC
        return (pz * NY + y, x * NC + pc), pz * NC + pc

    peers_a = [peer_a(o) for o in A_OFFS]
    peers_b = [peer_b(o) for o in B_OFFS]

    loads = []
    for n in range(PAIRS):
        loads.append((
            pltpu.make_async_copy(tok_hbm.at[n], tok_v.at[n], in_sem.at[0, n]),
            pltpu.make_async_copy(pat_hbm.at[n], pat_v.at[n], in_sem.at[1, n]),
        ))
        loads[-1][0].start()
        loads[-1][1].start()

    barrier = pltpu.get_barrier_semaphore()
    for (dev_a, _), (dev_b, _) in zip(peers_a, peers_b):
        pl.semaphore_signal(barrier, inc=1, device_id=dev_a, device_id_type=MESH)
        pl.semaphore_signal(barrier, inc=1, device_id=dev_b, device_id_type=MESH)

    def exchange(phase, src_a, dst_a, src_b, dst_b):
        copies = []
        for k in range(GROUP - 1):
            for side, peers, src, dst in ((0, peers_a, src_a, dst_a), (1, peers_b, src_b, dst_b)):
                dev, slot = peers[k]
                copies.append(pltpu.make_async_remote_copy(
                    src_ref=src(slot), dst_ref=dst,
                    send_sem=send_sem.at[phase, side, k], recv_sem=recv_sem.at[phase, side, k],
                    device_id=dev, device_id_type=MESH))
        for c in copies:
            c.start()
        return copies

    img_unit, img_inv = unit_rows(img_ref[...])
    txt_unit, txt_inv = unit_rows(txt_ref[...])
    img_half = img_unit.astype(BF16)
    txt_half = txt_unit.astype(BF16)
    matches = GLOBAL_SCALE * jnp.sum(
        jnp.sum(img_half.astype(F32) * txt_half.astype(F32), 1, keepdims=True), 0, keepdims=True)
    for half, dst in ((img_half, half_a), (txt_half, half_b)):
        wide_half = half.astype(F32)
        for c in range(CH):
            stage[pl.ds(c, PAIRS, stride=CH), :] = wide_half[:, c * 128:(c + 1) * 128]
        dst[...] = stage[...].astype(BF16)

    fine_refs = (s_ref, q_ref, hi_ref, lo_ref, wb_ref, wq_ref, z_ref, e_ref, bp_ref, v_ref,
                 x1_ref, d_ref, col_ref, ds_out, m_out, c_out)

    def run_pair(n):
        pltpu.make_async_copy(tok_hbm.at[n], tok_v.at[n], in_sem.at[0, n]).wait()
        pltpu.make_async_copy(pat_hbm.at[n], pat_v.at[n], in_sem.at[1, n]).wait()
        return fine_pair(n, len_ref[n], tok_v.at[n], pat_v.at[n], *fine_refs)

    fine_ref[...] = jnp.zeros_like(fine_ref)

    def step(n, carry):
        fine_ref[0:1, 0:1] += run_pair(n)
        return carry

    lax.fori_loop(0, 1, step, 0)
    pl.semaphore_wait(barrier, 2 * (GROUP - 1))

    own_a = pl.multiple_of(u * SLOT, SLOT)
    own_b = pl.multiple_of(v * SLOT, SLOT)
    first = exchange(
        0, lambda slot: half_a, unit_a.at[pl.ds(own_a, SLOT)],
        lambda slot: half_b, unit_b.at[pl.ds(own_b, SLOT)])
    unit_a[pl.ds(own_a, SLOT), :] = half_a[...]
    unit_b[pl.ds(own_b, SLOT), :] = half_b[...]

    lax.fori_loop(1, PAIRS, step, 0)
    for c in first:
        c.wait()

    for src, dst in ((unit_a, mat_a), (unit_b, mat_b)):
        wide[...] = src[...].astype(F32)
        for c in range(CH):
            dst[:, c * 128:(c + 1) * 128] = wide[pl.ds(c, ROWS, stride=CH), :].astype(BF16)

    logits = GLOBAL_SCALE * dot_nt(mat_a[...], mat_b[...])
    turned = GLOBAL_SCALE * dot_nt(mat_b[...], mat_a[...])
    scalar = fine_ref[0:1, 0:1] - matches
    for block, dst, row in ((turned, stat_a, u), (logits, stat_b, v)):
        top = jnp.max(block, 0, keepdims=True)
        dst[row, 0:1, 0:ROWS] = top
        dst[row, 1:2, 0:ROWS] = jnp.sum(jnp.exp(block - top), 0, keepdims=True)
        dst[row, 2:3, :] = jnp.broadcast_to(scalar, (1, 128))
    second = exchange(
        1, lambda slot: stat_a.at[u], stat_a.at[u], lambda slot: stat_b.at[v], stat_b.at[v])
    for c in second:
        c.wait()

    def combine(stat):
        top = stat[0, 0:1, 0:ROWS]
        for k in range(1, GROUP):
            top = jnp.maximum(top, stat[k, 0:1, 0:ROWS])
        total = jnp.zeros((1, ROWS), F32)
        for k in range(GROUP):
            total = total + stat[k, 1:2, 0:ROWS] * jnp.exp(stat[k, 0:1, 0:ROWS] - top)
        return top + jnp.log(total)

    row_lse = combine(stat_a)
    col_lse = combine(stat_b)
    fine_sum = stat_a[0, 2:3, 0:1]
    for k in range(1, GROUP):
        fine_sum = fine_sum + stat_a[k, 2:3, 0:1]
    tell_b[...] = jnp.broadcast_to(
        fine_sum + 0.5 * jnp.sum(row_lse, 1, keepdims=True), tell_b.shape)
    tell_a[...] = jnp.broadcast_to(0.5 * jnp.sum(col_lse, 1, keepdims=True), tell_a.shape)

    i_at = lax.broadcasted_iota(jnp.int32, (ROWS, ROWS), 0)
    j_at = lax.broadcasted_iota(jnp.int32, (ROWS, ROWS), 1)

    def same(img_at, txt_at):
        off = img_at - PAIRS * u
        inside = jnp.logical_and(off >= 0, off < PAIRS)
        return jnp.where(jnp.logical_and(inside, off == txt_at - PAIRS * v), 0.5, 0.0)

    row_part = (0.5 * jnp.exp(turned - row_lse) - same(j_at, i_at)).astype(BF16)
    col_part = (0.5 * jnp.exp(logits - col_lse) - same(i_at, j_at)).astype(BF16)
    for c in range(CH):
        cols = slice(c * 128, (c + 1) * 128)
        txt_c = mat_b[:, cols]
        img_c = mat_a[:, cols]
        part_a[pl.ds(c, ROWS, stride=CH), :] = dot_tn(row_part, txt_c) + dot_nn(col_part, txt_c)
        part_b[pl.ds(c, ROWS, stride=CH), :] = dot_nn(row_part, img_c) + dot_tn(col_part, img_c)

    def piece(ref):
        return lambda slot: ref.at[pl.ds(pl.multiple_of(slot * SLOT, SLOT), SLOT)]

    third = exchange(
        2, piece(part_a), got_a.at[pl.ds(own_a, SLOT)], piece(part_b), got_b.at[pl.ds(own_b, SLOT)])
    notes = exchange(3, lambda slot: tell_a, note_a.at[u], lambda slot: tell_b, note_b.at[v])
    got_a[pl.ds(own_a, SLOT), :] = part_a[pl.ds(own_a, SLOT), :]
    got_b[pl.ds(own_b, SLOT), :] = part_b[pl.ds(own_b, SLOT), :]
    note_a[u] = tell_a[...]
    note_b[v] = tell_b[...]
    for c in third:
        c.wait()
    for c in notes:
        c.wait()

    for got, unit, inv, out in ((got_a, img_unit, img_inv, gimg_out), (got_b, txt_unit, txt_inv, gtxt_out)):
        total = got[0:SLOT, :]
        for k in range(1, GROUP):
            total = total + got[k * SLOT:(k + 1) * SLOT, :]
        stage[...] = GLOBAL_SCALE * total
        along = jnp.zeros((PAIRS, 1), F32)
        for c in range(CH):
            along = along + jnp.sum(
                stage[pl.ds(c, PAIRS, stride=CH), :] * unit[:, c * 128:(c + 1) * 128], 1, keepdims=True)
        for c in range(CH):
            cols = slice(c * 128, (c + 1) * 128)
            part = stage[pl.ds(c, PAIRS, stride=CH), :]
            out[:, cols] = ((part - unit[:, cols] * along) * inv).astype(BF16)
    total = note_a[0, 0:1, 0:1] + note_b[0, 0:1, 0:1]
    for k in range(1, GROUP):
        total = total + note_a[k, 0:1, 0:1] + note_b[k, 0:1, 0:1]
    loss_out[...] = total * (1.0 / (GROUP * GROUP * PAIRS))


def apply_kernel(tok_ref, pat_ref, ds_ref, m_ref, c_ref, gimg_ref, gtxt_ref, loss_ref,
                 gtok_out, gpat_out, gimg_out, gtxt_out, loss_out):
    ds = ds_ref[0]
    m = m_ref[0]
    c = c_ref[0]
    for k in range(D // 256):
        cols = slice(k * 256, (k + 1) * 256)
        tok = tok_ref[0, :, cols]
        pat = pat_ref[0, :, cols]
        gtok_out[0, :, cols] = (dot_nn(ds, pat) + c * tok.astype(F32)).astype(BF16)
        gpat_out[0, :, cols] = (dot_tn(ds, tok) + dot_nn(m, pat)).astype(BF16)
    gimg_out[...] = gimg_ref[...]
    gtxt_out[...] = gtxt_ref[...]
    loss_out[...] = loss_ref[...]


def body(tokens, patches, lengths, img_pooled, txt_pooled):
    vmem = pl.BlockSpec(memory_space=pltpu.VMEM)
    smem = pl.BlockSpec(memory_space=pltpu.SMEM)
    hbm = pl.BlockSpec(memory_space=pl.ANY)
    sds = jax.ShapeDtypeStruct
    vm = pltpu.VMEM
    ds, m, c, gimg, gtxt, loss = pl.pallas_call(
        exchange_kernel,
        name="exchange",
        out_shape=(
            sds((PAIRS, T, T), BF16), sds((PAIRS, T, T), BF16), sds((PAIRS, T, 1), F32),
            sds((PAIRS, D), BF16), sds((PAIRS, D), BF16), sds((1, 1), F32)),
        in_specs=[smem, hbm, hbm, vmem, vmem],
        out_specs=(vmem,) * 6,
        scratch_shapes=[
            vm((PAIRS, T, D), BF16), vm((PAIRS, T, D), BF16),
            vm((T, T), F32), vm((T, T), BF16), vm((T, T), BF16), vm((T, T), BF16), vm((T, T), BF16),
            vm((T, T), F32), vm((T, T), F32), vm((T, T), F32), vm((T, T), BF16), vm((T, T), BF16),
            vm((T, T), F32), vm((T, T), F32), vm((T, 128), F32),
            vm((SLOT, 128), F32), vm((GROUP * SLOT, 128), BF16), vm((GROUP * SLOT, 128), BF16),
            vm((ROWS, D), BF16), vm((ROWS, D), BF16), vm((GROUP * SLOT, 128), F32),
            vm((SLOT, 128), BF16), vm((SLOT, 128), BF16),
            vm((GROUP * SLOT, 128), F32), vm((GROUP * SLOT, 128), F32),
            vm((GROUP, 4, 128), F32), vm((GROUP, 4, 128), F32), vm((1, ROWS), F32), vm((1, ROWS), F32),
            vm((GROUP * SLOT, 128), F32), vm((GROUP * SLOT, 128), F32),
            vm((GROUP, 1, 128), F32), vm((GROUP, 1, 128), F32), vm((1, 128), F32), vm((1, 128), F32),
            vm((8, 128), F32),
            pltpu.SemaphoreType.DMA((2, PAIRS)),
            pltpu.SemaphoreType.DMA((4, 2, GROUP - 1)),
            pltpu.SemaphoreType.DMA((4, 2, GROUP - 1)),
        ],
        compiler_params=pltpu.CompilerParams(
            collective_id=0, has_side_effects=True, vmem_limit_bytes=56 << 20),
    )(lengths, tokens, patches, img_pooled, txt_pooled)

    def block(*shape):
        return pl.BlockSpec((1,) + shape, lambda n: (n,) + (0,) * len(shape))

    def fixed(*shape):
        return pl.BlockSpec(shape, lambda n: (0,) * len(shape))

    gtok, gpat, gimg, gtxt, loss = pl.pallas_call(
        apply_kernel,
        name="apply",
        grid=(PAIRS,),
        out_shape=(
            sds((PAIRS, T, D), BF16), sds((PAIRS, T, D), BF16),
            sds((PAIRS, D), BF16), sds((PAIRS, D), BF16), sds((1, 1), F32)),
        in_specs=[block(T, D), block(T, D), block(T, T), block(T, T), block(T, 1),
                  fixed(PAIRS, D), fixed(PAIRS, D), fixed(1, 1)],
        out_specs=(block(T, D), block(T, D), fixed(PAIRS, D), fixed(PAIRS, D), fixed(1, 1)),
        compiler_params=pltpu.CompilerParams(
            dimension_semantics=("arbitrary",), vmem_limit_bytes=32 << 20),
    )(tokens, patches, ds, m, c, gimg, gtxt, loss)
    return gtok, gpat, gimg, gtxt, loss.reshape(())


def solution(mesh):
    both = ("dp", "grp")
    placed = (P(both, None, None), P(both, None, None), P(both), P(both, None), P(both, None))
    return jax.shard_map(
        body,
        mesh=mesh,
        in_specs=placed,
        out_specs=(P(both, None, None), P(both, None, None), P(both, None), P(both, None), P()),
        check_vma=False,
    )
```

```python
import functools

import jax
import jax.numpy as jnp
from jax import lax
from jax.experimental import pallas as pl
from jax.experimental.pallas import tpu as pltpu
from jax.sharding import PartitionSpec as P

MESH = pl.DeviceIdType.MESH
F32 = jnp.float32
BF16 = jnp.bfloat16

RANGE_EPS = 1e-06
NORM_EPS = 1e-06
GLOBAL_SCALE = 100.0
FINE_SCALE = 50.0

NX, NY, NZ, NC = 4, 4, 8, 2
GROUP = 16
D = 1024
CH = D // 128
PAIRS = 4
ROWS = GROUP * PAIRS
SLOT = PAIRS * CH
T = 256
LOG2_E = 1.4426950408889634


def dot_nn(a, b):
    return lax.dot_general(a, b, (((1,), (0,)), ((), ())), preferred_element_type=F32)


def dot_nt(a, b):
    return lax.dot_general(a, b, (((1,), (1,)), ((), ())), preferred_element_type=F32)


def dot_tn(a, b):
    return lax.dot_general(a, b, (((0,), (0,)), ((), ())), preferred_element_type=F32)


def ring(d, n):
    return min(d, n - d)


A_OFFS = sorted(
    ((dx, dy) for dx in range(NX) for dy in range(NY) if (dx, dy) != (0, 0)),
    key=lambda o: -(ring(o[0], NX) + ring(o[1], NY)),
)
B_OFFS = sorted(
    ((dz, dc) for dz in range(NZ) for dc in range(NC) if (dz, dc) != (0, 0)),
    key=lambda o: -ring(o[0], NZ),
)


def fine_losses(pair, length, tok, pat, st, hi, lo, wb, wq, zt, et, bp, m, rowv, colv):
    st[pair] = dot_nt(pat[...], tok[...])
    q = dot_nt(pat[...], pat[...]).astype(BF16)
    squares = tok[...] * tok[...]
    norm = dot_nn(squares, jnp.ones((D, 128), BF16))
    ti = lax.rsqrt(norm + NORM_EPS)
    inv_len = 0.5 / jnp.full((1, 1), length, jnp.int32).astype(F32)

    for h in range(2):
        cols = slice(h * 128, (h + 1) * 128)
        s = st[pair, :, cols]
        low = jnp.min(s, 0, keepdims=True)
        high = jnp.max(s, 0, keepdims=True)
        inv = 1.0 / (high - low + RANGE_EPS)
        raw = jnp.maximum((s - low) * inv - 1.0 / T, 0.0)
        iw = 1.0 / jnp.sum(raw, 0, keepdims=True)
        wb[pair, :, cols] = (raw * iw).astype(BF16)
        top = s.astype(BF16)
        hi[pair, :, cols] = top
        lo[pair, :, cols] = (s - top.astype(F32)).astype(BF16)
        rowv[pair, 0:1, cols] = low
        rowv[pair, 1:2, cols] = high
        rowv[pair, 2:3, cols] = inv
        rowv[pair, 3:4, cols] = iw

    wq[pair] = dot_nn(q, wb[pair])
    zt[...] = dot_tn(hi[pair], wb[pair]) + dot_tn(lo[pair], wb[pair])

    k_at = lax.broadcasted_iota(jnp.int32, (T, 1), 0)
    t_at = lax.broadcasted_iota(jnp.int32, (1, T), 1)
    scale_k = ti * (FINE_SCALE * LOG2_E)
    over_t = jnp.zeros((T, 128), F32)
    loss = jnp.zeros((1, 1), F32)
    for h in range(2):
        cols = slice(h * 128, (h + 1) * 128)
        ok = t_at[:, cols] < length
        gg = jnp.sum(wb[pair, :, cols].astype(F32) * wq[pair, :, cols], 0, keepdims=True)
        gi = lax.rsqrt(jnp.maximum(gg, 0.0) + NORM_EPS)
        z = zt[:, cols] * scale_k * gi
        e = jnp.where(jnp.logical_and(k_at < length, ok), jnp.exp2(z), 0.0)
        zt[:, cols] = z
        et[:, cols] = e
        rs = jnp.sum(e, 0, keepdims=True)
        over_t = over_t + e
        rowv[pair, 4:5, cols] = gi
        rowv[pair, 5:6, cols] = jnp.where(ok, 1.0 / rs, 0.0)
        loss = loss + jnp.sum(jnp.where(ok, jnp.log(rs), 0.0), 1, keepdims=True)
    cs = jnp.sum(over_t, 1, keepdims=True)
    k_ok = k_at < length
    loss = loss + jnp.sum(jnp.where(k_ok, jnp.log(cs), 0.0), 0, keepdims=True)
    ic = jnp.where(k_ok, 1.0 / cs, 0.0)

    bp_k = ti * (FINE_SCALE * inv_len)
    over_t = [jnp.zeros((128, 128), F32)] * 2
    for h in range(2):
        cols = slice(h * 128, (h + 1) * 128)
        gi = rowv[pair, 4:5, cols]
        ir = rowv[pair, 5:6, cols]
        r = jnp.zeros((1, 128), F32)
        for b in range(2):
            rows = slice(b * 128, (b + 1) * 128)
            z = zt[rows, cols]
            g = et[rows, cols] * (ir + ic[rows, :])
            if b == h:
                own = k_at[rows, :] == t_at[:, cols]
                both = jnp.logical_and(own, t_at[:, cols] < length)
                g = g - jnp.where(both, 2.0, 0.0)
                diag = jnp.sum(jnp.where(both, z, 0.0), 0, keepdims=True)
                loss = loss - (2.0 / LOG2_E) * jnp.sum(diag, 1, keepdims=True)
            prod = g * z
            r = r + jnp.sum(prod, 0, keepdims=True)
            over_t[b] = over_t[b] + prod
            bp[pair, rows, cols] = (g * gi * bp_k[rows, :]).astype(BF16)
        coef = gi * gi * r * (inv_len / LOG2_E)
        rowv[pair, 6:7, cols] = coef
        et[:, cols] = wb[pair, :, cols].astype(F32) * (-coef)
    for b in range(2):
        rows = slice(b * 128, (b + 1) * 128)
        along = jnp.sum(over_t[b], 1, keepdims=True) * (inv_len / LOG2_E)
        colv[pair, rows, :] = (-along * ti[rows, :] * ti[rows, :]).astype(BF16)
    m[pair] = dot_nt(et[...].astype(BF16), wb[pair]).astype(BF16)
    return loss * inv_len


def fine_grads(pair, tok, pat, st, hi, lo, wb, wq, x1, d, bp, ds, m, rowv, colv, gtok, gpat):
    x1[...] = dot_nn(hi[pair], bp[pair]) + dot_nn(lo[pair], bp[pair])
    d[...] = dot_nt(wb[pair], bp[pair])
    for h in range(2):
        cols = slice(h * 128, (h + 1) * 128)
        low = rowv[pair, 0:1, cols]
        high = rowv[pair, 1:2, cols]
        inv = rowv[pair, 2:3, cols]
        iw = rowv[pair, 3:4, cols]
        coef = rowv[pair, 6:7, cols]
        s = st[pair, :, cols]
        x = (s - low) * inv - 1.0 / T
        w = jnp.maximum(x, 0.0) * iw
        dw = x1[:, cols] - coef * wq[pair, :, cols]
        mean = jnp.sum(dw * w, 0, keepdims=True)
        slope = iw * inv
        gate = jnp.where(x > 0.0, slope, jnp.where(x == 0.0, 0.5 * slope, 0.0))
        a = gate * (dw - mean)
        total = jnp.sum(a, 0, keepdims=True)
        at_high = s == high
        at_low = s == low
        n_high = jnp.sum(jnp.where(at_high, 1.0, 0.0), 0, keepdims=True)
        n_low = jnp.sum(jnp.where(at_low, 1.0, 0.0), 0, keepdims=True)
        to_high = total * (-1.0 / T) / n_high
        to_low = total * (1.0 / T - 1.0) / n_low
        ends = jnp.where(at_high, to_high, jnp.where(at_low, to_low, 0.0))
        ds[:, cols] = (a + ends + d[:, cols]).astype(BF16)
    c = jnp.concatenate([colv[pair], colv[pair]], 1)
    for k in range(D // 256):
        cols = slice(k * 256, (k + 1) * 256)
        gtok[pair, :, cols] = dot_tn(ds[...], pat[:, cols]).astype(BF16) + c * tok[:, cols]
        gpat[pair, :, cols] = (dot_nn(ds[...], tok[:, cols]) + dot_nn(m[pair], pat[:, cols])).astype(BF16)


def unit_rows(pooled):
    values = pooled.astype(F32)
    inverse = lax.rsqrt(jnp.sum(values * values, 1, keepdims=True) + NORM_EPS)
    return values * inverse, inverse


def exchange_kernel(len_hbm, tok_hbm, pat_hbm, img_hbm, txt_hbm,
                    gtok_out, gpat_out, gimg_out, gtxt_out, loss_out,
                    tok_v, pat_v, st, hi, lo, wb, wq, zt, et, bp, ds, m, rowv, colv,
                    stage, unit_a, unit_b, mat_a, mat_b, wide, half_a, half_b, part_a, part_b,
                    whole_a, whole_b, stat_a, stat_b, got_a, got_b, note_a, note_b, tell_a, tell_b,
                    fine_ref, len_ref, img_ref, txt_ref, in_sem, small_sem, send_sem, recv_sem):
    dp = lax.axis_index("dp")
    grp = lax.axis_index("grp")
    z, y = dp // NY, dp % NY
    x, core = grp // NC, grp % NC
    u = y * NX + x
    v = z * NC + core

    def peer_a(off):
        px, py = (x + off[0]) % NX, (y + off[1]) % NY
        return (z * NY + py, px * NC + core), py * NX + px

    def peer_b(off):
        pz, pc = (z + off[0]) % NZ, (core + off[1]) % NC
        return (pz * NY + y, x * NC + pc), pz * NC + pc

    peers_a = [peer_a(o) for o in A_OFFS]
    peers_b = [peer_b(o) for o in B_OFFS]

    small = [pltpu.make_async_copy(src, dst, small_sem.at[k]) for k, (src, dst) in enumerate(
        ((len_hbm, len_ref), (img_hbm, img_ref), (txt_hbm, txt_ref)))]
    for c in small:
        c.start()
    loads = []
    for n in range(PAIRS):
        loads.append((
            pltpu.make_async_copy(tok_hbm.at[n], tok_v.at[n], in_sem.at[0, n]),
            pltpu.make_async_copy(pat_hbm.at[n], pat_v.at[n], in_sem.at[1, n]),
        ))
        loads[-1][0].start()
        loads[-1][1].start()

    barrier = pltpu.get_barrier_semaphore()
    for (dev_a, _), (dev_b, _) in zip(peers_a, peers_b):
        pl.semaphore_signal(barrier, inc=1, device_id=dev_a, device_id_type=MESH)
        pl.semaphore_signal(barrier, inc=1, device_id=dev_b, device_id_type=MESH)

    def exchange(phase, src_a, dst_a, src_b, dst_b):
        copies = []
        for k in range(GROUP - 1):
            for side, peers, src, dst in ((0, peers_a, src_a, dst_a), (1, peers_b, src_b, dst_b)):
                dev, slot = peers[k]
                copies.append(pltpu.make_async_remote_copy(
                    src_ref=src(slot), dst_ref=dst,
                    send_sem=send_sem.at[phase, side, k], recv_sem=recv_sem.at[phase, side, k],
                    device_id=dev, device_id_type=MESH))
        for c in copies:
            c.start()
        return copies

    for c in small:
        c.wait()
    img_unit, img_inv = unit_rows(img_ref[...])
    txt_unit, txt_inv = unit_rows(txt_ref[...])
    img_half = img_unit.astype(BF16)
    txt_half = txt_unit.astype(BF16)
    matches = GLOBAL_SCALE * jnp.sum(
        jnp.sum(img_half.astype(F32) * txt_half.astype(F32), 1, keepdims=True), 0, keepdims=True)
    for half, dst in ((img_half, half_a), (txt_half, half_b)):
        wide_half = half.astype(F32)
        for c in range(CH):
            stage[pl.ds(c, PAIRS, stride=CH), :] = wide_half[:, c * 128:(c + 1) * 128]
        dst[...] = stage[...].astype(BF16)

    def losses(n, carry):
        pltpu.make_async_copy(tok_hbm.at[n], tok_v.at[n], in_sem.at[0, n]).wait()
        pltpu.make_async_copy(pat_hbm.at[n], pat_v.at[n], in_sem.at[1, n]).wait()
        fine_ref[0:1, 0:1] += fine_losses(
            n, len_ref[n], tok_v.at[n], pat_v.at[n], st, hi, lo, wb, wq, zt, et, bp, m, rowv, colv)
        return carry

    def grads(n, carry):
        fine_grads(n, tok_v.at[n], pat_v.at[n], st, hi, lo, wb, wq, zt, et, bp, ds, m, rowv, colv,
                   gtok_out, gpat_out)
        return carry

    fine_ref[...] = jnp.zeros_like(fine_ref)
    lax.fori_loop(0, 1, losses, 0)
    pl.semaphore_wait(barrier, 2 * (GROUP - 1))

    own_a = pl.multiple_of(u * SLOT, SLOT)
    own_b = pl.multiple_of(v * SLOT, SLOT)
    first = exchange(
        0, lambda slot: half_a, unit_a.at[pl.ds(own_a, SLOT)],
        lambda slot: half_b, unit_b.at[pl.ds(own_b, SLOT)])
    unit_a[pl.ds(own_a, SLOT), :] = half_a[...]
    unit_b[pl.ds(own_b, SLOT), :] = half_b[...]

    lax.fori_loop(1, PAIRS, losses, 0)
    for c in first:
        c.wait()

    for src, dst in ((unit_a, mat_a), (unit_b, mat_b)):
        wide[...] = src[...].astype(F32)
        for c in range(CH):
            dst[:, c * 128:(c + 1) * 128] = wide[pl.ds(c, ROWS, stride=CH), :].astype(BF16)

    logits = GLOBAL_SCALE * dot_nt(mat_a[...], mat_b[...])
    turned = GLOBAL_SCALE * dot_nt(mat_b[...], mat_a[...])
    scalar = fine_ref[0:1, 0:1] - matches
    for block, dst, row in ((turned, stat_a, u), (logits, stat_b, v)):
        top = jnp.max(block, 0, keepdims=True)
        dst[row, 0:1, 0:ROWS] = top
        dst[row, 1:2, 0:ROWS] = jnp.sum(jnp.exp(block - top), 0, keepdims=True)
        dst[row, 2:3, :] = jnp.broadcast_to(scalar, (1, 128))
    second = exchange(
        1, lambda slot: stat_a.at[u], stat_a.at[u], lambda slot: stat_b.at[v], stat_b.at[v])
    lax.fori_loop(0, 2, grads, 0)
    for c in second:
        c.wait()

    def combine(stat):
        top = stat[0, 0:1, 0:ROWS]
        for k in range(1, GROUP):
            top = jnp.maximum(top, stat[k, 0:1, 0:ROWS])
        total = jnp.zeros((1, ROWS), F32)
        for k in range(GROUP):
            total = total + stat[k, 1:2, 0:ROWS] * jnp.exp(stat[k, 0:1, 0:ROWS] - top)
        return top + jnp.log(total)

    row_lse = combine(stat_a)
    col_lse = combine(stat_b)
    fine_sum = stat_a[0, 2:3, 0:1]
    for k in range(1, GROUP):
        fine_sum = fine_sum + stat_a[k, 2:3, 0:1]
    lane_at = lax.broadcasted_iota(jnp.int32, (1, 128), 1)
    say_b = fine_sum + 0.5 * jnp.sum(row_lse, 1, keepdims=True)
    say_a = 0.5 * jnp.sum(col_lse, 1, keepdims=True)

    i_at = lax.broadcasted_iota(jnp.int32, (ROWS, ROWS), 0)
    j_at = lax.broadcasted_iota(jnp.int32, (ROWS, ROWS), 1)

    def same(img_at, txt_at):
        off = img_at - PAIRS * u
        inside = jnp.logical_and(off >= 0, off < PAIRS)
        return jnp.where(jnp.logical_and(inside, off == txt_at - PAIRS * v), 0.5, 0.0)

    row_part = (0.5 * jnp.exp(turned - row_lse) - same(j_at, i_at)).astype(BF16)
    col_part = (0.5 * jnp.exp(logits - col_lse) - same(i_at, j_at)).astype(BF16)
    for c in range(D // 256):
        cols = slice(c * 256, (c + 1) * 256)
        txt_c = mat_b[:, cols]
        img_c = mat_a[:, cols]
        whole_a[:, cols] = dot_tn(row_part, txt_c) + dot_nn(col_part, txt_c)
        whole_b[:, cols] = dot_nn(row_part, img_c) + dot_tn(col_part, img_c)
    diag = lax.broadcasted_iota(jnp.int32, (ROWS, 128), 0) == lax.broadcasted_iota(jnp.int32, (ROWS, 128), 1)
    for whole, mat, part, tell, say in (
            (whole_a, mat_a, part_a, tell_a, say_a), (whole_b, mat_b, part_b, tell_b, say_b)):
        along = jnp.zeros((ROWS, 128), F32)
        for c in range(CH):
            cols = slice(c * 128, (c + 1) * 128)
            along = along + whole[:, cols] * mat[:, cols].astype(F32)
        along = jnp.sum(along, 1, keepdims=True)
        for c in range(CH):
            cols = slice(c * 128, (c + 1) * 128)
            wide[pl.ds(c, ROWS, stride=CH), :] = whole[:, cols] - along * mat[:, cols].astype(F32)
        part[...] = wide[...].astype(BF16)
        row = jnp.sum(jnp.where(diag, along, 0.0), 0, keepdims=True)
        tell[...] = jnp.where(lane_at < ROWS, row, say)

    def piece(ref):
        return lambda slot: ref.at[pl.ds(pl.multiple_of(slot * SLOT, SLOT), SLOT)]

    third = exchange(
        2, piece(part_a), got_a.at[pl.ds(own_a, SLOT)], piece(part_b), got_b.at[pl.ds(own_b, SLOT)])
    notes = exchange(3, lambda slot: tell_a, note_a.at[u], lambda slot: tell_b, note_b.at[v])
    got_a[pl.ds(own_a, SLOT), :] = part_a[pl.ds(own_a, SLOT), :]
    got_b[pl.ds(own_b, SLOT), :] = part_b[pl.ds(own_b, SLOT), :]
    note_a[u] = tell_a[...]
    note_b[v] = tell_b[...]
    lax.fori_loop(2, PAIRS, grads, 0)
    for c in third:
        c.wait()
    for c in notes:
        c.wait()

    loss = jnp.zeros((1, 1), F32)
    for got, note, slot, unit, half, inv, out in (
            (got_a, note_a, u, img_unit, img_half, img_inv, gimg_out),
            (got_b, note_b, v, txt_unit, txt_half, txt_inv, gtxt_out)):
        total = got[0:SLOT, :].astype(F32)
        told = note[0]
        for k in range(1, GROUP):
            total = total + got[k * SLOT:(k + 1) * SLOT, :].astype(F32)
            told = told + note[k]
        loss = loss + told[:, ROWS:ROWS + 1]
        own = lane_at == PAIRS * slot + lax.broadcasted_iota(jnp.int32, (PAIRS, 128), 0)
        lead = jnp.sum(jnp.where(own, told, 0.0), 1, keepdims=True)
        stage[...] = total
        rows = [GLOBAL_SCALE * (stage[pl.ds(c, PAIRS, stride=CH), :]
                                + lead * half[:, c * 128:(c + 1) * 128].astype(F32)) for c in range(CH)]
        along = jnp.zeros((PAIRS, 1), F32)
        for c in range(CH):
            along = along + jnp.sum(rows[c] * unit[:, c * 128:(c + 1) * 128], 1, keepdims=True)
        for c in range(CH):
            cols = slice(c * 128, (c + 1) * 128)
            out[:, cols] = ((rows[c] - unit[:, cols] * along) * inv).astype(BF16)
    loss_out[...] = loss * (1.0 / (GROUP * GROUP * PAIRS))


def store_kernel(gtok_ref, gpat_ref, gimg_ref, gtxt_ref, loss_ref,
                 gtok_out, gpat_out, gimg_out, gtxt_out, loss_out, sem):
    copies = []
    for n in range(PAIRS):
        copies.append(pltpu.make_async_copy(gtok_ref.at[n], gtok_out.at[n], sem.at[0, n]))
        copies.append(pltpu.make_async_copy(gpat_ref.at[n], gpat_out.at[n], sem.at[1, n]))
    for c in copies:
        c.start()
    gimg_out[...] = gimg_ref[...]
    gtxt_out[...] = gtxt_ref[...]
    loss_out[...] = loss_ref[...]
    for c in copies:
        c.wait()


def body(tokens, patches, lengths, img_pooled, txt_pooled):
    vmem = pl.BlockSpec(memory_space=pltpu.VMEM)
    hbm = pl.BlockSpec(memory_space=pltpu.HBM)
    sds = jax.ShapeDtypeStruct
    vm = pltpu.VMEM
    square = (PAIRS, T, T)
    gtok, gpat, gimg, gtxt, loss = pl.pallas_call(
        exchange_kernel,
        name="exchange",
        out_shape=(
            vm((PAIRS, T, D), BF16), vm((PAIRS, T, D), BF16),
            vm((PAIRS, D), BF16), vm((PAIRS, D), BF16), vm((1, 1), F32)),
        in_specs=[hbm] * 5,
        out_specs=(vmem,) * 5,
        scratch_shapes=[
            vm((PAIRS, T, D), BF16), vm((PAIRS, T, D), BF16),
            vm(square, F32), vm(square, BF16), vm(square, BF16), vm(square, BF16), vm(square, F32),
            vm((T, T), F32), vm((T, T), F32), vm(square, BF16), vm((T, T), BF16), vm(square, BF16),
            vm((PAIRS, 8, T), F32), vm((PAIRS, T, 128), BF16),
            vm((SLOT, 128), F32), vm((GROUP * SLOT, 128), BF16), vm((GROUP * SLOT, 128), BF16),
            vm((ROWS, D), BF16), vm((ROWS, D), BF16), vm((GROUP * SLOT, 128), F32),
            vm((SLOT, 128), BF16), vm((SLOT, 128), BF16),
            vm((GROUP * SLOT, 128), BF16), vm((GROUP * SLOT, 128), BF16),
            vm((ROWS, D), F32), vm((ROWS, D), F32),
            vm((GROUP, 4, 128), F32), vm((GROUP, 4, 128), F32),
            vm((GROUP * SLOT, 128), BF16), vm((GROUP * SLOT, 128), BF16),
            vm((GROUP, 1, 128), F32), vm((GROUP, 1, 128), F32), vm((1, 128), F32), vm((1, 128), F32),
            vm((8, 128), F32), pltpu.SMEM((PAIRS,), jnp.int32), vm((PAIRS, D), BF16), vm((PAIRS, D), BF16),
            pltpu.SemaphoreType.DMA((2, PAIRS)), pltpu.SemaphoreType.DMA((3,)),
            pltpu.SemaphoreType.DMA((4, 2, GROUP - 1)),
            pltpu.SemaphoreType.DMA((4, 2, GROUP - 1)),
        ],
        compiler_params=pltpu.CompilerParams(
            collective_id=0, has_side_effects=True, vmem_limit_bytes=40 << 20),
    )(*(pltpu.with_memory_space_constraint(a, pltpu.HBM)
        for a in (lengths, tokens, patches, img_pooled, txt_pooled)))

    gtok, gpat, gimg, gtxt, loss = pl.pallas_call(
        store_kernel,
        name="store",
        out_shape=(
            sds((PAIRS, T, D), BF16), sds((PAIRS, T, D), BF16),
            sds((PAIRS, D), BF16), sds((PAIRS, D), BF16), sds((1, 1), F32)),
        in_specs=[vmem] * 5,
        out_specs=(hbm, hbm, vmem, vmem, vmem),
        scratch_shapes=[pltpu.SemaphoreType.DMA((2, PAIRS))],
        compiler_params=pltpu.CompilerParams(vmem_limit_bytes=32 << 20),
    )(gtok, gpat, gimg, gtxt, loss)
    return gtok, gpat, gimg, gtxt, loss.reshape(())


def solution(mesh):
    both = ("dp", "grp")
    placed = (P(both, None, None), P(both, None, None), P(both), P(both, None), P(both, None))
    return jax.shard_map(
        body,
        mesh=mesh,
        in_specs=placed,
        out_specs=(P(both, None, None), P(both, None, None), P(both, None), P(both, None), P()),
        check_vma=False,
    )
```

```python
import functools

import jax
import jax.numpy as jnp
from jax import lax
from jax.experimental import pallas as pl
from jax.experimental.pallas import tpu as pltpu
from jax.sharding import PartitionSpec as P

MESH = pl.DeviceIdType.MESH
F32 = jnp.float32
BF16 = jnp.bfloat16

RANGE_EPS = 1e-06
NORM_EPS = 1e-06
GLOBAL_SCALE = 100.0
FINE_SCALE = 50.0

NX, NY, NZ, NC = 4, 4, 8, 2
GROUP = 16
D = 1024
CH = D // 128
PAIRS = 4
ROWS = GROUP * PAIRS
SLOT = PAIRS * CH
T = 256
LOG2_E = 1.4426950408889634


def dot_nn(a, b):
    return lax.dot_general(a, b, (((1,), (0,)), ((), ())), preferred_element_type=F32)


def dot_nt(a, b):
    return lax.dot_general(a, b, (((1,), (1,)), ((), ())), preferred_element_type=F32)


def dot_tn(a, b):
    return lax.dot_general(a, b, (((0,), (0,)), ((), ())), preferred_element_type=F32)


def ring(d, n):
    return min(d, n - d)


A_OFFS = sorted(
    ((dx, dy) for dx in range(NX) for dy in range(NY) if (dx, dy) != (0, 0)),
    key=lambda o: -(ring(o[0], NX) + ring(o[1], NY)),
)
B_OFFS = sorted(
    ((dz, dc) for dz in range(NZ) for dc in range(NC) if (dz, dc) != (0, 0)),
    key=lambda o: -ring(o[0], NZ),
)


def fine_losses(pair, length, tok, pat, st, hi, lo, wb, wq, zt, et, bp, m, rowv, colv):
    st[pair] = dot_nt(pat[...], tok[...])
    q = dot_nt(pat[...], pat[...]).astype(BF16)
    squares = tok[...] * tok[...]
    norm = dot_nn(squares, jnp.ones((D, 128), BF16))
    ti = lax.rsqrt(norm + NORM_EPS)
    inv_len = 0.5 / jnp.full((1, 1), length, jnp.int32).astype(F32)

    for h in range(2):
        cols = slice(h * 128, (h + 1) * 128)
        s = st[pair, :, cols]
        low = jnp.min(s, 0, keepdims=True)
        high = jnp.max(s, 0, keepdims=True)
        inv = 1.0 / (high - low + RANGE_EPS)
        raw = jnp.maximum((s - low) * inv - 1.0 / T, 0.0)
        iw = 1.0 / jnp.sum(raw, 0, keepdims=True)
        wb[pair, :, cols] = (raw * iw).astype(BF16)
        top = s.astype(BF16)
        hi[pair, :, cols] = top
        lo[pair, :, cols] = (s - top.astype(F32)).astype(BF16)
        rowv[pair, 0:1, cols] = low
        rowv[pair, 1:2, cols] = high
        rowv[pair, 2:3, cols] = inv
        rowv[pair, 3:4, cols] = iw

    wq[pair] = dot_nn(q, wb[pair])
    zt[...] = dot_tn(hi[pair], wb[pair]) + dot_tn(lo[pair], wb[pair])

    k_at = lax.broadcasted_iota(jnp.int32, (T, 1), 0)
    t_at = lax.broadcasted_iota(jnp.int32, (1, T), 1)
    scale_k = ti * (FINE_SCALE * LOG2_E)
    over_t = jnp.zeros((T, 128), F32)
    loss = jnp.zeros((1, 1), F32)
    for h in range(2):
        cols = slice(h * 128, (h + 1) * 128)
        ok = t_at[:, cols] < length
        gg = jnp.sum(wb[pair, :, cols].astype(F32) * wq[pair, :, cols], 0, keepdims=True)
        gi = lax.rsqrt(jnp.maximum(gg, 0.0) + NORM_EPS)
        z = zt[:, cols] * scale_k * gi
        e = jnp.where(jnp.logical_and(k_at < length, ok), jnp.exp2(z), 0.0)
        zt[:, cols] = z
        et[:, cols] = e
        rs = jnp.sum(e, 0, keepdims=True)
        over_t = over_t + e
        rowv[pair, 4:5, cols] = gi
        rowv[pair, 5:6, cols] = jnp.where(ok, 1.0 / rs, 0.0)
        loss = loss + jnp.sum(jnp.where(ok, jnp.log(rs), 0.0), 1, keepdims=True)
    cs = jnp.sum(over_t, 1, keepdims=True)
    k_ok = k_at < length
    loss = loss + jnp.sum(jnp.where(k_ok, jnp.log(cs), 0.0), 0, keepdims=True)
    ic = jnp.where(k_ok, 1.0 / cs, 0.0)

    bp_k = ti * (FINE_SCALE * inv_len)
    over_t = [jnp.zeros((128, 128), F32)] * 2
    for h in range(2):
        cols = slice(h * 128, (h + 1) * 128)
        gi = rowv[pair, 4:5, cols]
        ir = rowv[pair, 5:6, cols]
        r = jnp.zeros((1, 128), F32)
        for b in range(2):
            rows = slice(b * 128, (b + 1) * 128)
            z = zt[rows, cols]
            g = et[rows, cols] * (ir + ic[rows, :])
            if b == h:
                own = k_at[rows, :] == t_at[:, cols]
                both = jnp.logical_and(own, t_at[:, cols] < length)
                g = g - jnp.where(both, 2.0, 0.0)
                diag = jnp.sum(jnp.where(both, z, 0.0), 0, keepdims=True)
                loss = loss - (2.0 / LOG2_E) * jnp.sum(diag, 1, keepdims=True)
            prod = g * z
            r = r + jnp.sum(prod, 0, keepdims=True)
            over_t[b] = over_t[b] + prod
            bp[pair, rows, cols] = (g * gi * bp_k[rows, :]).astype(BF16)
        coef = gi * gi * r * (inv_len / LOG2_E)
        rowv[pair, 6:7, cols] = coef
        et[:, cols] = wb[pair, :, cols].astype(F32) * (-coef)
    for b in range(2):
        rows = slice(b * 128, (b + 1) * 128)
        along = jnp.sum(over_t[b], 1, keepdims=True) * (inv_len / LOG2_E)
        colv[pair, rows, :] = (-along * ti[rows, :] * ti[rows, :]).astype(BF16)
    m[pair] = dot_nt(et[...].astype(BF16), wb[pair]).astype(BF16)
    return loss * inv_len


def fine_grads(pair, tok, pat, st, hi, lo, wb, wq, x1, d, bp, ds, m, rowv, colv, gtok, gpat):
    x1[...] = dot_nn(hi[pair], bp[pair]) + dot_nn(lo[pair], bp[pair])
    d[...] = dot_nt(wb[pair], bp[pair])
    for h in range(2):
        cols = slice(h * 128, (h + 1) * 128)
        low = rowv[pair, 0:1, cols]
        high = rowv[pair, 1:2, cols]
        inv = rowv[pair, 2:3, cols]
        iw = rowv[pair, 3:4, cols]
        coef = rowv[pair, 6:7, cols]
        s = st[pair, :, cols]
        x = (s - low) * inv - 1.0 / T
        w = jnp.maximum(x, 0.0) * iw
        dw = x1[:, cols] - coef * wq[pair, :, cols]
        mean = jnp.sum(dw * w, 0, keepdims=True)
        slope = iw * inv
        gate = jnp.where(x > 0.0, slope, jnp.where(x == 0.0, 0.5 * slope, 0.0))
        a = gate * (dw - mean)
        total = jnp.sum(a, 0, keepdims=True)
        at_high = s == high
        at_low = s == low
        n_high = jnp.sum(jnp.where(at_high, 1.0, 0.0), 0, keepdims=True)
        n_low = jnp.sum(jnp.where(at_low, 1.0, 0.0), 0, keepdims=True)
        to_high = total * (-1.0 / T) / n_high
        to_low = total * (1.0 / T - 1.0) / n_low
        ends = jnp.where(at_high, to_high, jnp.where(at_low, to_low, 0.0))
        ds[:, cols] = (a + ends + d[:, cols]).astype(BF16)
    c = jnp.concatenate([colv[pair], colv[pair]], 1)
    for k in range(D // 256):
        cols = slice(k * 256, (k + 1) * 256)
        gtok[pair, :, cols] = dot_tn(ds[...], pat[:, cols]).astype(BF16) + c * tok[:, cols]
        gpat[pair, :, cols] = (dot_nn(ds[...], tok[:, cols]) + dot_nn(m[pair], pat[:, cols])).astype(BF16)


def unit_rows(pooled):
    values = pooled.astype(F32)
    inverse = lax.rsqrt(jnp.sum(values * values, 1, keepdims=True) + NORM_EPS)
    return values * inverse, inverse


def exchange_kernel(len_hbm, tok_hbm, pat_hbm, img_hbm, txt_hbm,
                    gtok_out, gpat_out, gimg_out, gtxt_out, loss_out,
                    tok_v, pat_v, st, hi, lo, wb, wq, zt, et, bp, ds, m, rowv, colv,
                    stage, unit_a, unit_b, mat_a, mat_b, wide, half_a, half_b, part_a, part_b,
                    whole_a, whole_b, stat_a, stat_b, got_a, got_b, note_a, note_b, tell_a, tell_b,
                    fine_ref, len_ref, img_ref, txt_ref, in_sem, small_sem, send_sem, recv_sem):
    dp = lax.axis_index("dp")
    grp = lax.axis_index("grp")
    z, y = dp // NY, dp % NY
    x, core = grp // NC, grp % NC
    u = y * NX + x
    v = z * NC + core

    def peer_a(off):
        px, py = (x + off[0]) % NX, (y + off[1]) % NY
        return (z * NY + py, px * NC + core), py * NX + px

    def peer_b(off):
        pz, pc = (z + off[0]) % NZ, (core + off[1]) % NC
        return (pz * NY + y, x * NC + pc), pz * NC + pc

    peers_a = [peer_a(o) for o in A_OFFS]
    peers_b = [peer_b(o) for o in B_OFFS]

    small = [pltpu.make_async_copy(src, dst, small_sem.at[k]) for k, (src, dst) in enumerate(
        ((len_hbm, len_ref), (img_hbm, img_ref), (txt_hbm, txt_ref)))]
    for c in small:
        c.start()
    def load(n):
        pltpu.make_async_copy(tok_hbm.at[n], tok_v.at[n], in_sem.at[0, n]).start()
        pltpu.make_async_copy(pat_hbm.at[n], pat_v.at[n], in_sem.at[1, n]).start()

    load(0)
    barrier = pltpu.get_barrier_semaphore()
    for (dev_a, _), (dev_b, _) in zip(peers_a, peers_b):
        pl.semaphore_signal(barrier, inc=1, device_id=dev_a, device_id_type=MESH)
        pl.semaphore_signal(barrier, inc=1, device_id=dev_b, device_id_type=MESH)

    def exchange(phase, side, peers, src, dst):
        for dev, slot in peers:
            pltpu.make_async_remote_copy(
                src_ref=src(slot), dst_ref=dst,
                send_sem=send_sem.at[phase, side], recv_sem=recv_sem.at[phase, side],
                device_id=dev, device_id_type=MESH).start()

    def arrived(phase, side, many):
        pltpu.make_async_copy(many, many, recv_sem.at[phase, side]).wait()

    def sent(phase, side, many):
        pltpu.make_async_copy(many, many, send_sem.at[phase, side]).wait()

    peer_rows = pl.ds(0, (GROUP - 1) * SLOT)
    peer_slots = pl.ds(0, GROUP - 1)

    for c in small:
        c.wait()
    img_unit, img_inv = unit_rows(img_ref[...])
    txt_unit, txt_inv = unit_rows(txt_ref[...])
    img_half = img_unit.astype(BF16)
    txt_half = txt_unit.astype(BF16)
    matches = GLOBAL_SCALE * jnp.sum(
        jnp.sum(img_half.astype(F32) * txt_half.astype(F32), 1, keepdims=True), 0, keepdims=True)
    for half, dst in ((img_half, half_a), (txt_half, half_b)):
        wide_half = half.astype(F32)
        for c in range(CH):
            stage[pl.ds(c, PAIRS, stride=CH), :] = wide_half[:, c * 128:(c + 1) * 128]
        dst[...] = stage[...].astype(BF16)

    def losses(n, carry):
        pltpu.make_async_copy(tok_hbm.at[n], tok_v.at[n], in_sem.at[0, n]).wait()
        pltpu.make_async_copy(pat_hbm.at[n], pat_v.at[n], in_sem.at[1, n]).wait()
        fine_ref[0:1, 0:1] += fine_losses(
            n, len_ref[n], tok_v.at[n], pat_v.at[n], st, hi, lo, wb, wq, zt, et, bp, m, rowv, colv)
        return carry

    def grads(n, carry):
        fine_grads(n, tok_v.at[n], pat_v.at[n], st, hi, lo, wb, wq, zt, et, bp, ds, m, rowv, colv,
                   gtok_out, gpat_out)
        return carry

    own_a = pl.multiple_of(u * SLOT, SLOT)
    own_b = pl.multiple_of(v * SLOT, SLOT)
    fine_ref[...] = jnp.zeros_like(fine_ref)
    unit_a[pl.ds(own_a, SLOT), :] = half_a[...]
    unit_b[pl.ds(own_b, SLOT), :] = half_b[...]

    def load_next(n, carry):
        load(n)
        return carry

    lax.fori_loop(1, PAIRS, load_next, 0)
    pl.semaphore_wait(barrier, 2 * (GROUP - 1))
    exchange(0, 1, peers_b, lambda slot: half_b, unit_b.at[pl.ds(own_b, SLOT)])
    exchange(0, 0, peers_a, lambda slot: half_a, unit_a.at[pl.ds(own_a, SLOT)])
    lax.fori_loop(0, PAIRS, losses, 0)
    arrived(0, 0, unit_a.at[peer_rows])
    arrived(0, 1, unit_b.at[peer_rows])

    for src, dst in ((unit_a, mat_a), (unit_b, mat_b)):
        wide[...] = src[...].astype(F32)
        for c in range(CH):
            dst[:, c * 128:(c + 1) * 128] = wide[pl.ds(c, ROWS, stride=CH), :].astype(BF16)

    logits = GLOBAL_SCALE * dot_nt(mat_a[...], mat_b[...])
    turned = GLOBAL_SCALE * dot_nt(mat_b[...], mat_a[...])
    scalar = fine_ref[0:1, 0:1] - matches
    for block, dst, row in ((turned, stat_a, u), (logits, stat_b, v)):
        top = jnp.max(block, 0, keepdims=True)
        dst[row, 0:1, 0:ROWS] = top
        dst[row, 1:2, 0:ROWS] = jnp.sum(jnp.exp(block - top), 0, keepdims=True)
        dst[row, 2:3, :] = jnp.broadcast_to(scalar, (1, 128))
    exchange(1, 1, peers_b, lambda slot: stat_b.at[v], stat_b.at[v])
    exchange(1, 0, peers_a, lambda slot: stat_a.at[u], stat_a.at[u])
    lax.fori_loop(0, 2, grads, 0)
    arrived(1, 0, stat_a.at[peer_slots])
    arrived(1, 1, stat_b.at[peer_slots])

    def combine(stat):
        top = stat[0, 0:1, 0:ROWS]
        for k in range(1, GROUP):
            top = jnp.maximum(top, stat[k, 0:1, 0:ROWS])
        total = jnp.zeros((1, ROWS), F32)
        for k in range(GROUP):
            total = total + stat[k, 1:2, 0:ROWS] * jnp.exp(stat[k, 0:1, 0:ROWS] - top)
        return top + jnp.log(total)

    row_lse = combine(stat_a)
    col_lse = combine(stat_b)
    fine_sum = stat_a[0, 2:3, 0:1]
    for k in range(1, GROUP):
        fine_sum = fine_sum + stat_a[k, 2:3, 0:1]
    lane_at = lax.broadcasted_iota(jnp.int32, (1, 128), 1)
    say_b = fine_sum + 0.5 * jnp.sum(row_lse, 1, keepdims=True)
    say_a = 0.5 * jnp.sum(col_lse, 1, keepdims=True)

    i_at = lax.broadcasted_iota(jnp.int32, (ROWS, ROWS), 0)
    j_at = lax.broadcasted_iota(jnp.int32, (ROWS, ROWS), 1)

    def same(img_at, txt_at):
        off = img_at - PAIRS * u
        inside = jnp.logical_and(off >= 0, off < PAIRS)
        return jnp.where(jnp.logical_and(inside, off == txt_at - PAIRS * v), 0.5, 0.0)

    row_part = (0.5 * jnp.exp(turned - row_lse) - same(j_at, i_at)).astype(BF16)
    col_part = (0.5 * jnp.exp(logits - col_lse) - same(i_at, j_at)).astype(BF16)
    diag = lax.broadcasted_iota(jnp.int32, (ROWS, 128), 0) == lax.broadcasted_iota(jnp.int32, (ROWS, 128), 1)

    def piece(ref):
        return lambda slot: ref.at[pl.ds(pl.multiple_of(slot * SLOT, SLOT), SLOT)]

    def partials(other, mat, whole, part, tell, say, turn):
        for c in range(D // 256):
            cols = slice(c * 256, (c + 1) * 256)
            far = other[:, cols]
            if turn:
                whole[:, cols] = dot_tn(row_part, far) + dot_nn(col_part, far)
            else:
                whole[:, cols] = dot_nn(row_part, far) + dot_tn(col_part, far)
        along = jnp.zeros((ROWS, 128), F32)
        for c in range(CH):
            cols = slice(c * 128, (c + 1) * 128)
            along = along + whole[:, cols] * mat[:, cols].astype(F32)
        along = jnp.sum(along, 1, keepdims=True)
        for c in range(CH):
            cols = slice(c * 128, (c + 1) * 128)
            wide[pl.ds(c, ROWS, stride=CH), :] = whole[:, cols] - along * mat[:, cols].astype(F32)
        part[...] = wide[...].astype(BF16)
        row = jnp.sum(jnp.where(diag, along, 0.0), 0, keepdims=True)
        tell[...] = jnp.where(lane_at < ROWS, row, say)

    partials(mat_a, mat_b, whole_b, part_b, tell_b, say_b, False)
    partials(mat_b, mat_a, whole_a, part_a, tell_a, say_a, True)
    got_a[pl.ds(own_a, SLOT), :] = part_a[pl.ds(own_a, SLOT), :]
    got_b[pl.ds(own_b, SLOT), :] = part_b[pl.ds(own_b, SLOT), :]
    note_a[u] = tell_a[...]
    note_b[v] = tell_b[...]
    exchange(2, 1, peers_b, piece(part_b), got_b.at[pl.ds(own_b, SLOT)])
    exchange(2, 0, peers_a, piece(part_a), got_a.at[pl.ds(own_a, SLOT)])
    exchange(3, 1, peers_b, lambda _: tell_b, note_b.at[v])
    exchange(3, 0, peers_a, lambda _: tell_a, note_a.at[u])
    lax.fori_loop(2, PAIRS, grads, 0)
    for side, unit, stat, got, note in ((0, unit_a, stat_a, got_a, note_a), (1, unit_b, stat_b, got_b, note_b)):
        sent(0, side, unit.at[peer_rows])
        sent(1, side, stat.at[peer_slots])
        sent(2, side, got.at[peer_rows])
        sent(3, side, note.at[peer_slots])
        arrived(2, side, got.at[peer_rows])
        arrived(3, side, note.at[peer_slots])

    loss = jnp.zeros((1, 1), F32)
    for got, note, slot, unit, half, inv, out in (
            (got_a, note_a, u, img_unit, img_half, img_inv, gimg_out),
            (got_b, note_b, v, txt_unit, txt_half, txt_inv, gtxt_out)):
        total = got[0:SLOT, :].astype(F32)
        told = note[0]
        for k in range(1, GROUP):
            total = total + got[k * SLOT:(k + 1) * SLOT, :].astype(F32)
            told = told + note[k]
        loss = loss + told[:, ROWS:ROWS + 1]
        own = lane_at == PAIRS * slot + lax.broadcasted_iota(jnp.int32, (PAIRS, 128), 0)
        lead = jnp.sum(jnp.where(own, told, 0.0), 1, keepdims=True)
        stage[...] = total
        rows = [GLOBAL_SCALE * (stage[pl.ds(c, PAIRS, stride=CH), :]
                                + lead * half[:, c * 128:(c + 1) * 128].astype(F32)) for c in range(CH)]
        along = jnp.zeros((PAIRS, 1), F32)
        for c in range(CH):
            along = along + jnp.sum(rows[c] * unit[:, c * 128:(c + 1) * 128], 1, keepdims=True)
        for c in range(CH):
            cols = slice(c * 128, (c + 1) * 128)
            out[:, cols] = ((rows[c] - unit[:, cols] * along) * inv).astype(BF16)
    loss_out[...] = jnp.broadcast_to(loss * (1.0 / (GROUP * GROUP * PAIRS)), loss_out.shape)


def store_kernel(gtok_ref, gpat_ref, gimg_ref, gtxt_ref, loss_ref,
                 gtok_out, gpat_out, gimg_out, gtxt_out, loss_out, one, sem):
    copies = []
    for n in range(PAIRS):
        copies.append(pltpu.make_async_copy(gtok_ref.at[n], gtok_out.at[n], sem.at[0, n]))
        copies.append(pltpu.make_async_copy(gpat_ref.at[n], gpat_out.at[n], sem.at[1, n]))
    copies.append(pltpu.make_async_copy(gimg_ref, gimg_out, sem.at[2, 0]))
    copies.append(pltpu.make_async_copy(gtxt_ref, gtxt_out, sem.at[2, 1]))
    copies.append(pltpu.make_async_copy(one, loss_out, sem.at[2, 2]))
    one[...] = loss_ref[0:1, 0:1]
    for c in copies:
        c.start()
    for c in copies:
        c.wait()


def body(tokens, patches, lengths, img_pooled, txt_pooled):
    vmem = pl.BlockSpec(memory_space=pltpu.VMEM)
    hbm = pl.BlockSpec(memory_space=pltpu.HBM)
    sds = jax.ShapeDtypeStruct
    vm = pltpu.VMEM
    square = (PAIRS, T, T)
    gtok, gpat, gimg, gtxt, loss = pl.pallas_call(
        exchange_kernel,
        name="exchange",
        out_shape=(
            vm((PAIRS, T, D), BF16), vm((PAIRS, T, D), BF16),
            vm((PAIRS, D), BF16), vm((PAIRS, D), BF16), vm((8, 128), F32)),
        in_specs=[hbm] * 5,
        out_specs=(vmem,) * 5,
        scratch_shapes=[
            vm((PAIRS, T, D), BF16), vm((PAIRS, T, D), BF16),
            vm(square, F32), vm(square, BF16), vm(square, BF16), vm(square, BF16), vm(square, F32),
            vm((T, T), F32), vm((T, T), F32), vm(square, BF16), vm((T, T), BF16), vm(square, BF16),
            vm((PAIRS, 8, T), F32), vm((PAIRS, T, 128), BF16),
            vm((SLOT, 128), F32), vm((GROUP * SLOT, 128), BF16), vm((GROUP * SLOT, 128), BF16),
            vm((ROWS, D), BF16), vm((ROWS, D), BF16), vm((GROUP * SLOT, 128), F32),
            vm((SLOT, 128), BF16), vm((SLOT, 128), BF16),
            vm((GROUP * SLOT, 128), BF16), vm((GROUP * SLOT, 128), BF16),
            vm((ROWS, D), F32), vm((ROWS, D), F32),
            vm((GROUP, 4, 128), F32), vm((GROUP, 4, 128), F32),
            vm((GROUP * SLOT, 128), BF16), vm((GROUP * SLOT, 128), BF16),
            vm((GROUP, 1, 128), F32), vm((GROUP, 1, 128), F32), vm((1, 128), F32), vm((1, 128), F32),
            vm((8, 128), F32), pltpu.SMEM((PAIRS,), jnp.int32), vm((PAIRS, D), BF16), vm((PAIRS, D), BF16),
            pltpu.SemaphoreType.DMA((2, PAIRS)), pltpu.SemaphoreType.DMA((3,)),
            pltpu.SemaphoreType.DMA((4, 2)),
            pltpu.SemaphoreType.DMA((4, 2)),
        ],
        compiler_params=pltpu.CompilerParams(
            collective_id=0, has_side_effects=True, vmem_limit_bytes=40 << 20),
    )(*(pltpu.with_memory_space_constraint(a, pltpu.HBM)
        for a in (lengths, tokens, patches, img_pooled, txt_pooled)))

    gtok, gpat, gimg, gtxt, loss = pl.pallas_call(
        store_kernel,
        name="store",
        out_shape=(
            sds((PAIRS, T, D), BF16), sds((PAIRS, T, D), BF16),
            sds((PAIRS, D), BF16), sds((PAIRS, D), BF16), sds((1, 1), F32)),
        in_specs=[vmem] * 5,
        out_specs=(hbm,) * 5,
        scratch_shapes=[vm((1, 1), F32), pltpu.SemaphoreType.DMA((3, PAIRS))],
        compiler_params=pltpu.CompilerParams(vmem_limit_bytes=32 << 20),
    )(gtok, gpat, gimg, gtxt, loss)
    return gtok, gpat, gimg, gtxt, loss.reshape(())


def solution(mesh):
    both = ("dp", "grp")
    placed = (P(both, None, None), P(both, None, None), P(both), P(both, None), P(both, None))
    return jax.shard_map(
        body,
        mesh=mesh,
        in_specs=placed,
        out_specs=(P(both, None, None), P(both, None, None), P(both, None), P(both, None), P()),
        check_vma=False,
    )
```
